512 devices in a mesh: vol: 128 (over y, z, core), rep: 4 (over x).
Axes of the slice: x: 4, y: 8, z: 8, core: 2. Of those that a mesh axis runs over, the one named last changes fastest.
Arguments:
- surface_state: float32 [14336, 32, 128], P('vol', 'rep'), may hold values from -6 to 6
- direction: float32 [14336, 32, 128], P('vol', 'rep'), may hold values from -6 to 6
- stiffness: float32 [14336, 128], P('vol'), may hold values from 0.5 to 5
- partners: int32 [14336, 4], P('vol'), may hold values from 0 to 14335, as said below
- contact_owner: int32 [14336], P('vol'), may hold values from 0 to 127, as said below
- projection: float32 [32, 32], replicated, may hold values from -1 to 1
- mortar: float32 [4, 128, 128], replicated, may hold values from -0.5 to 0.5
Outputs:
- hessian_product: float32 [14336, 32, 128], P('vol', 'rep')
The draws below stay inside these ranges and needn't reach their ends.
Inputs may be any that keep to these rules, and one draw needn't show every extreme that they name: `contact_owner`: in the 112 blocks of one volume owner (aligned blocks of rows) no contact owner is named more than 2 times; 14 contact owners are named exactly 2 times in every such block. `partners`: partners may repeat, may be the block itself, and may have another contact owner than their block.
All inputs are finite; a program needn't handle non-finite values.
Results may differ from the reference program's by a relative error of at most 0.0001.
Values sent between devices are 32-bit elements; how exact they have to be, the bound alone decides.
A program may use at most 64 MiB of HBM per device.

```python
import math
import jax
import jax.numpy as jnp
from jax import lax

FACES = 128
CHANNELS = 32
PARTNERS = 4
BLK_DEV = 112
NB = 14336
CAP = 2
HOT = 14
N_VOL = 128


def route_table(key):
    folded = jax.random.fold_in(key, 7)
    key_hot, key_len, key_score, key_block = jax.random.split(folded, 4)
    half_cap = (CAP + 1) // 2
    hot_order = jax.random.permutation(key_hot, N_VOL).astype(jnp.int32)
    hot_rank = jnp.argsort(hot_order).astype(jnp.int32)
    is_cold = (hot_rank >= HOT).astype(jnp.int32)
    dest_iota = jnp.arange(N_VOL, dtype=jnp.int32)
    scores = jax.random.randint(key_score, (N_VOL, N_VOL), 0, 1024)
    sort_keys = (is_cold[None, :] * 1024 + scores) * N_VOL + dest_iota[None, :]
    dest_order = jnp.argsort(sort_keys, axis=1).astype(jnp.int32)
    lengths = jax.random.randint(key_len, (N_VOL, N_VOL), half_cap, CAP + 1)
    lengths = jnp.where(dest_iota[None, :] < HOT, CAP, lengths)
    run_ends = jnp.cumsum(lengths, axis=1)
    positions = jnp.arange(BLK_DEV, dtype=jnp.int32)
    groups = jnp.sum((run_ends[:, None, :] <= positions[None, :, None]).astype(jnp.int32), axis=2)
    targets = jnp.take_along_axis(dest_order, groups, axis=1)
    block_scores = jax.random.randint(key_block, (N_VOL, BLK_DEV), 0, 1024) * BLK_DEV + positions[None, :]
    shuffled = jnp.argsort(block_scores, axis=1).astype(jnp.int32)
    inverse = jnp.argsort(shuffled, axis=1).astype(jnp.int32)
    owners = jnp.take_along_axis(targets, inverse, axis=1)
    return owners.reshape(NB).astype(jnp.int32)


def draw_contact_owner(key, part):
    return route_table(key)


def draw_partners(key, part):
    owners = route_table(key)
    sorted_blocks = jnp.argsort(owners, stable=True).astype(jnp.int32)
    counts = jax.ops.segment_sum(jnp.ones(NB, jnp.int32), owners, num_segments=N_VOL)
    starts = jnp.cumsum(counts) - counts
    drawn_picks = jax.random.randint(jax.random.fold_in(key, 11), (NB, PARTNERS), 0, 1 << 20)
    drawn_picks = drawn_picks % counts[owners][:, None]
    local_picks = sorted_blocks[starts[owners][:, None] + drawn_picks].astype(jnp.int32)
    cross_picks = jax.random.randint(jax.random.fold_in(key, 13), (NB, PARTNERS), 0, NB).astype(jnp.int32)
    flags = jax.random.randint(jax.random.fold_in(key, 17), (NB, PARTNERS), 0, 8)
    return jnp.where(flags == 0, cross_picks, local_picks).astype(jnp.int32)


def levels(own_key, shape, shards, smallest, largest):
    factor_of, own = 1.0, jax.random.fold_in(own_key, 6)
    for position, blocks in shards:
        heights = jnp.exp(jax.random.uniform(jax.random.fold_in(own, position), (blocks,), jnp.float32, smallest / len(shards), largest / len(shards)))
        factor_of = factor_of * jnp.repeat(heights, shape[position] // blocks).reshape([-1 if axis == position else 1 for axis in range(len(shape))])
    return factor_of


def normal_values(own_key, shape, spread, limit, cuts=(), kind=jnp.bfloat16):
    drawn = spread * jax.random.normal(own_key, shape, jnp.float32)
    if cuts:
        drawn = drawn * levels(own_key, shape, cuts, -0.22, 0.18)
    return jnp.clip(drawn, -limit, limit).astype(kind)


def setup_inputs(seed: int = 0) -> dict:
    seeds = jax.random.split(jax.random.key(seed), 8)
    surface_state = normal_values(seeds[0], (NB, CHANNELS, FACES), 1.0, 6.0, ((0, 128), (1, 4)), jnp.float32)
    direction = normal_values(seeds[1], (NB, CHANNELS, FACES), 1.0, 6.0, ((0, 128), (1, 4)), jnp.float32)
    stiffness = jnp.clip(jnp.exp(math.log(5.0) - 2.3025851 * jax.random.uniform(seeds[2], (NB, FACES), jnp.float32) ** levels(seeds[2], (NB, FACES), ((0, 128),), -0.2, 0.2)), 0.5, 5.0)
    partners = draw_partners(jax.random.fold_in(seeds[7], 71), 0)
    contact_owner = draw_contact_owner(jax.random.fold_in(seeds[7], 71), 0)
    projection = normal_values(seeds[5], (CHANNELS, CHANNELS), CHANNELS ** -0.5, 1.0, (), jnp.float32)
    mortar = normal_values(seeds[6], (PARTNERS, FACES, FACES), FACES ** -0.5, 0.5, (), jnp.float32)
    return dict(surface_state=surface_state, direction=direction, stiffness=stiffness, partners=partners, contact_owner=contact_owner, projection=projection, mortar=mortar)


sharpness = 1.5


def reference(surface_state, direction, stiffness, partners, contact_owner, projection, mortar):
    highest = lax.Precision.HIGHEST
    projected = jnp.einsum("ij,bjf->bif", projection, surface_state, precision=highest)
    moving = jnp.einsum("ij,bjf->bif", projection, direction, precision=highest)
    block_total = surface_state.shape[0]
    tangent = jnp.zeros_like(projected)
    returned = jnp.zeros_like(projected)
    for column in range(PARTNERS):
        target = partners[:, column].astype(jnp.int32)
        mapped_state = jnp.einsum("bcf,fg->bcg", projected[target], mortar[column], precision=highest)
        mapped_move = jnp.einsum("bcf,fg->bcg", moving[target], mortar[column], precision=highest)
        contact_gap = projected - mapped_state
        squashed = jax.nn.sigmoid(sharpness * contact_gap)
        agree = (contact_owner == contact_owner[target]).astype(jnp.float32)
        weight = agree[:, None, None] * stiffness[:, None, :] * sharpness * squashed * (1.0 - squashed)
        traction = weight * (moving - mapped_move)
        tangent = tangent + traction
        gathered_back = jax.ops.segment_sum(traction, target, num_segments=block_total)
        returned = returned + jnp.einsum("bcg,fg->bcf", gathered_back, mortar[column], precision=highest)
    summed = tangent - returned
    return jnp.einsum("ji,bjf->bif", projection, summed, precision=highest)
```

```python
import jax
import jax.numpy as jnp
from jax import lax
from jax.experimental import pallas as pl
from jax.experimental.pallas import tpu as pltpu
from jax.sharding import PartitionSpec as P

SHARPNESS = 1.5
BLOCKS = 112
CH = 8
FACES = 128
REPS = 4
NY = 8
NZC = 16
PARTNERS = 4
ROWS = BLOCKS * CH
HALF = ROWS // 2
F32 = jnp.float32
BF16 = jnp.bfloat16
MESH = pl.DeviceIdType.MESH


def split(x):
    high = x.astype(BF16)
    return high, (x - high.astype(F32)).astype(BF16)


def dot(a, b):
    return jnp.dot(a, b, preferred_element_type=F32)


def body(
    state,
    move,
    stiff_in,
    partners_in,
    owner_in,
    proj,
    mortar_in,
    out,
    gs,
    gd,
    orow,
    lab,
    sti,
    pick,
    pick_t,
    prj,
    mp0,
    mq0,
    ms0,
    mo0,
    mp1,
    mq1,
    ms1,
    mo1,
    labs,
    stis,
    g,
    gt,
    wfs,
    wts,
    mm,
    ml,
    mth,
    mtl,
    p0,
    q0,
    o0,
    p1,
    q1,
    o1,
    own,
    go,
    xs_send,
    xs_recv,
    x_local,
    c_send,
    c_recv,
    c_local,
):
    vol = lax.axis_index("vol")
    rep = lax.axis_index("rep")
    y = vol // NZC
    zc = lax.rem(vol, NZC)
    z = zc // 2
    core = lax.rem(zc, 2)
    right = lax.rem(rep + 1, REPS)
    left = lax.rem(rep + 3, REPS)

    def zc_peer(o):
        return lax.rem(z + o // 2, NY) * 2 + lax.rem(core + lax.rem(o, 2), 2)

    def y_peer(o):
        return lax.rem(y + o, NY)

    barrier = pltpu.get_barrier_semaphore()
    for side in (right, left):
        pl.semaphore_signal(barrier, inc=1, device_id=(vol, side), device_id_type=MESH)

    def greet_z(o, carry):
        peer = y * NZC + zc_peer(o)
        pl.semaphore_signal(barrier, inc=1, device_id=(peer, rep), device_id_type=MESH)
        return carry

    def greet_y(o, carry):
        peer = y_peer(o) * NZC + zc
        pl.semaphore_signal(barrier, inc=1, device_id=(peer, rep), device_id_type=MESH)
        return carry

    lax.fori_loop(1, NZC, greet_z, 0)
    lax.fori_loop(1, NY, greet_y, 0)
    pl.semaphore_wait(barrier, 2 + NZC - 1 + NY - 1)

    first = pl.ds(0, HALF)
    second = pl.ds(HALF, HALF)

    def x_copy(src, dst, n, index, side):
        copy = pltpu.make_async_remote_copy(
            src_ref=src,
            dst_ref=dst,
            send_sem=xs_send.at[n, index],
            recv_sem=xs_recv.at[n, index],
            device_id=(vol, side),
            device_id_type=MESH,
        )
        copy.start()
        return copy

    def x_start(src, dst, n):
        return [
            x_copy(src.at[first], dst.at[rep, first], n, 0, right),
            x_copy(src.at[second], dst.at[rep, second], n, 1, left),
            x_copy(src.at[second], dst.at[rep, second], n, 2, right),
            x_copy(src.at[first], dst.at[rep, first], n, 3, left),
        ]

    def x_relay(dst, n, copies):
        copies[0].wait_recv()
        copies.append(x_copy(dst.at[left, first], dst.at[left, first], n, 4, right))
        copies[1].wait_recv()
        copies.append(x_copy(dst.at[right, second], dst.at[right, second], n, 5, left))

    def x_finish(copies):
        for copy in copies[2:]:
            copy.wait_recv()

    def z_phase(src, dst, sem):
        def one(o, carry):
            peer = zc_peer(o)
            pltpu.make_async_remote_copy(
                src_ref=src(peer),
                dst_ref=dst(zc),
                send_sem=c_send.at[sem],
                recv_sem=c_recv.at[sem],
                device_id=(y * NZC + peer, rep),
                device_id_type=MESH,
            ).start()
            return carry

        lax.fori_loop(1, NZC, one, 0)
        local = pltpu.make_async_copy(src(zc), dst(zc), c_local.at[sem])
        local.start()
        return local

    def y_phase(src, dst, sem):
        def one(o, carry):
            peer = y_peer(o)
            pltpu.make_async_remote_copy(
                src_ref=src(peer),
                dst_ref=dst(y),
                send_sem=c_send.at[sem],
                recv_sem=c_recv.at[sem],
                device_id=(peer * NZC + zc, rep),
                device_id_type=MESH,
            ).start()
            return carry

        lax.fori_loop(1, NY, one, 0)
        local = pltpu.make_async_copy(src(y), dst(y), c_local.at[sem])
        local.start()
        return local

    def drain(local, ref, count, sem):
        whole = pltpu.make_async_remote_copy(
            src_ref=ref.at[pl.ds(0, count)],
            dst_ref=ref.at[pl.ds(0, count)],
            send_sem=c_send.at[sem],
            recv_sem=c_recv.at[sem],
            device_id=(vol, right),
            device_id_type=MESH,
        )
        local.wait()
        whole.wait_recv()
        whole.wait_send()

    copies_s = x_start(state, gs, 0)
    local_s = pltpu.make_async_copy(state, gs.at[rep], x_local.at[0])
    local_s.start()

    lane = lax.broadcasted_iota(jnp.int32, (128, 128), 1)
    row = lax.broadcasted_iota(jnp.int32, (128, 128), 0)
    orow[...] = jnp.full((8, 128), -1.0, F32)
    orow[0:1, 0:BLOCKS] = owner_in[...].astype(F32)
    across = jnp.broadcast_to(orow[0:1, :], (128, 128))
    down = across.T
    rank = jnp.sum(jnp.where((across == down) & (row < lane), 1.0, 0.0), axis=0, keepdims=True)
    dest0 = (lax.rem(row, NY) * NZC + row // NY).astype(F32)
    dest1 = row.astype(F32)
    pick0 = jnp.where((across == dest0) & (rank == 0.0), 1.0, 0.0)
    pick1 = jnp.where((across == dest1) & (rank == 1.0), 1.0, 0.0)
    pick[0:128, 0:128] = pick0.astype(BF16)
    pick[0:128, 128:256] = pick0.astype(BF16)
    pick[128:256, 0:128] = pick1.astype(BF16)
    pick[128:256, 128:256] = pick1.astype(BF16)
    pick_t[:, 0:128] = pick0.T.astype(BF16)
    pick_t[:, 128:256] = pick1.T.astype(BF16)

    lab[...] = jnp.zeros((128, 128), F32)
    lab[0:BLOCKS, 0:PARTNERS] = (partners_in[...] + 1).astype(F32)
    ids = lax.broadcasted_iota(jnp.int32, (BLOCKS, 1), 0) + (vol * BLOCKS + 1)
    lab[0:BLOCKS, PARTNERS : PARTNERS + 1] = ids.astype(F32)
    sti[...] = jnp.zeros((128, 128), F32)
    sti[0:BLOCKS, :] = stiff_in[...]

    def packed(x):
        high, low = split(x)
        return dot(pick[...], jnp.concatenate([high, low], axis=0))

    for kind, source in ((0, sti), (1, lab)):
        rows = packed(source[...])
        for i in range(NZC):
            mp0[i, kind] = rows[i * NY : (i + 1) * NY]
        for i in range(NY):
            mp1[i, kind] = rows[128 + i * NZC : 128 + (i + 1) * NZC]
    meta0 = z_phase(lambda i: mp0.at[i], lambda i: mq0.at[i], 0)
    meta1 = y_phase(lambda i: mp1.at[i], lambda i: mq1.at[i], 1)

    for k in range(PARTNERS):
        cols = slice(k * FACES, (k + 1) * FACES)
        high, low = split(mortar_in[k])
        mm[0:FACES, cols] = high
        mm[FACES : 2 * FACES, cols] = high
        ml[:, cols] = low
        high, low = split(mortar_in[k].T)
        mth[k, 0:FACES, :] = high
        mth[k, FACES : 2 * FACES, :] = high
        mtl[k] = low
    prj[...] = jnp.zeros((CH, 128, FACES), F32)

    x_relay(gs, 0, copies_s)
    copies_d = x_start(move, gd, 1)
    local_d = pltpu.make_async_copy(move, gd.at[rep], x_local.at[1])
    local_d.start()

    drain(meta0, mq0, NZC - 1, 0)
    drain(meta1, mq1, NY - 1, 1)
    flat0 = mq0.reshape(NZC * 2 * NY, FACES)
    flat1 = mq1.reshape(NY * 2 * NZC, FACES)
    for kind in range(2):
        for i in range(NY):
            ms0[i, kind] = flat0[pl.ds(kind * NY + i, NZC, stride=2 * NY), :]
        for i in range(NZC):
            ms1[i, kind] = flat1[pl.ds(kind * NZC + i, NY, stride=2 * NZC), :]
    meta0 = y_phase(lambda i: ms0.at[i], lambda i: mo0.at[i], 2)
    meta1 = z_phase(lambda i: ms1.at[i], lambda i: mo1.at[i], 3)

    def project(gathered, transposed):
        for start in (0, 56):
            for base in (0, 4):
                total = [jnp.zeros((56, FACES), F32) for _ in range(4)]
                for j in range(REPS * CH):
                    x = gathered[j // CH, pl.ds(start * CH + j % CH, 56, stride=CH), :]
                    for i in range(4):
                        if transposed:
                            factor = proj[j, rep * CH + base + i]
                        else:
                            factor = proj[rep * CH + base + i, j]
                        total[i] = total[i] + factor * x
                yield start, base, total

    def pack_field(gathered, n):
        for start, base, total in project(gathered, False):
            for i in range(4):
                prj[base + i, start : start + 56, :] = total[i]
        dst0 = p0.at[n].reshape(128 * CH, FACES)
        dst1 = p1.at[n].reshape(128 * CH, FACES)
        for i in range(CH):
            rows = packed(prj[i])
            dst0[pl.ds(i, 128, stride=CH), :] = rows[0:128]
            dst1[pl.ds(i, 128, stride=CH), :] = rows[128:256]

    def phase_one(n):
        sem = 4 + 4 * n
        a = z_phase(lambda i: p0.at[n, i], lambda i: q0.at[n, i], sem)
        b = y_phase(lambda i: p1.at[n, i], lambda i: q1.at[n, i], sem + 1)
        return a, b

    def phase_two(n, started):
        sem = 4 + 4 * n
        drain(started[0], q0.at[n], NZC - 1, sem)
        a = y_phase(lambda i: q0.at[n, :, i], lambda i: o0.at[n, i], sem + 2)
        drain(started[1], q1.at[n], NY - 1, sem + 1)
        b = z_phase(lambda i: q1.at[n, :, i], lambda i: o1.at[n, i], sem + 3)
        return a, b

    def phase_end(n, started):
        sem = 4 + 4 * n
        drain(started[0], o0.at[n], NY - 1, sem + 2)
        drain(started[1], o1.at[n], NZC - 1, sem + 3)

    x_finish(copies_s)
    local_s.wait()
    pack_field(gs, 0)
    run_s = phase_one(0)
    x_relay(gd, 1, copies_d)

    drain(meta0, mo0, NY - 1, 2)
    drain(meta1, mo1, NZC - 1, 3)
    for i in range(NY):
        stis[i * NZC : (i + 1) * NZC] = mo0[i, 0]
        labs[i * NZC : (i + 1) * NZC] = mo0[i, 1]
    for i in range(NZC):
        stis[128 + i * NY : 128 + (i + 1) * NY] = mo1[i, 0]
        labs[128 + i * NY : 128 + (i + 1) * NY] = mo1[i, 1]
    labels = labs[...]
    turned = labels.T
    ones = jnp.ones((256, FACES), BF16)
    for k in range(PARTNERS):
        hit = labels[:, k : k + 1] == turned[PARTNERS : PARTNERS + 1, :]
        g[k] = jnp.where(hit, 1.0, 0.0).astype(BF16)
        hit = labels[:, PARTNERS : PARTNERS + 1] == turned[k : k + 1, :]
        gt[k] = jnp.where(hit, 1.0, 0.0).astype(BF16)
        wfs[k] = dot(g[k], ones) * stis[...] * SHARPNESS

    run_s = phase_two(0, run_s)
    x_finish(copies_d)
    local_d.wait()
    pack_field(gd, 1)
    run_d = phase_one(1)
    phase_end(0, run_s)

    def received(n, i):
        a = o0.at[n].reshape(128 * CH, FACES)[pl.ds(i, 128, stride=CH), :]
        b = o1.at[n].reshape(128 * CH, FACES)[pl.ds(i, 128, stride=CH), :]
        return jnp.concatenate([a, b], axis=0)

    def mapped(x):
        high, low = split(x)
        total = dot(jnp.concatenate([high, low], axis=1), mm[...]) + dot(high, ml[...])
        result = []
        for k in range(PARTNERS):
            high, low = split(total[:, k * FACES : (k + 1) * FACES])
            both = dot(g[k], jnp.concatenate([high, low], axis=1))
            result.append(both[:, 0:FACES] + both[:, FACES:])
        return result

    def weigh(i, carry):
        x = received(0, i)
        for k, partner in enumerate(mapped(x)):
            squashed = 1.0 / (1.0 + jnp.exp(-SHARPNESS * (x - partner)))
            wts[i, k] = wfs[k] * squashed * (1.0 - squashed)
        return carry

    lax.fori_loop(0, CH, weigh, 0)
    run_d = phase_two(1, run_d)
    phase_end(1, run_d)

    back1 = p1.at[2].reshape(128 * CH, FACES)
    back0 = p0.at[2].reshape(128 * CH, FACES)

    def pull(i, carry):
        x = received(1, i)
        total = jnp.zeros((256, FACES), F32)
        for k, partner in enumerate(mapped(x)):
            traction = wts[i, k] * (x - partner)
            total = total + traction
            high, low = split(traction)
            both = dot(gt[k], jnp.concatenate([high, low], axis=1))
            high, low = split(both[:, 0:FACES] + both[:, FACES:])
            total = total - dot(jnp.concatenate([high, low], axis=1), mth[k]) - dot(high, mtl[k])
        back1[pl.ds(i, 128, stride=CH), :] = total[0:128]
        back0[pl.ds(i, 128, stride=CH), :] = total[128:256]
        return carry

    lax.fori_loop(0, CH, pull, 0)
    run_r = phase_one(2)
    run_r = phase_two(2, run_r)
    phase_end(2, run_r)

    home = own
    for i in range(CH):
        a = o1.at[2].reshape(128 * CH, FACES)[pl.ds(i, 128, stride=CH), :]
        b = o0.at[2].reshape(128 * CH, FACES)[pl.ds(i, 128, stride=CH), :]
        high, low = split(jnp.concatenate([a, b], axis=0))
        both = dot(pick_t[...], jnp.concatenate([high, low], axis=1))
        both = both[:, 0:FACES] + both[:, FACES:]
        home[pl.ds(i, BLOCKS, stride=CH), :] = both[0:BLOCKS]
    copies_o = x_start(own, go, 2)
    local_o = pltpu.make_async_copy(own, go.at[rep], x_local.at[2])
    local_o.start()
    x_relay(go, 2, copies_o)
    x_finish(copies_o)
    local_o.wait()
    for start, base, total in project(go, True):
        for i in range(4):
            out[pl.ds(start * CH + base + i, 56, stride=CH), :] = total[i]
    for copy in copies_s + copies_d + copies_o:
        copy.wait_send()


def local(surface_state, direction, stiffness, partners, contact_owner, projection, mortar):
    vmem = pl.BlockSpec(memory_space=pltpu.VMEM)
    anywhere = pl.BlockSpec(memory_space=pl.ANY)
    result = pl.pallas_call(
        body,
        out_shape=jax.ShapeDtypeStruct((ROWS, FACES), F32),
        in_specs=[
            anywhere,
            anywhere,
            vmem,
            vmem,
            vmem,
            pl.BlockSpec(memory_space=pltpu.SMEM),
            vmem,
        ],
        out_specs=vmem,
        scratch_shapes=[
            pltpu.VMEM((REPS, ROWS, FACES), F32),
            pltpu.VMEM((REPS, ROWS, FACES), F32),
            pltpu.VMEM((8, 128), F32),
            pltpu.VMEM((128, 128), F32),
            pltpu.VMEM((128, FACES), F32),
            pltpu.VMEM((256, 256), BF16),
            pltpu.VMEM((128, 256), BF16),
            pltpu.VMEM((CH, 128, FACES), F32),
            pltpu.VMEM((NZC, 2, NY, FACES), F32),
            pltpu.VMEM((NZC, 2, NY, FACES), F32),
            pltpu.VMEM((NY, 2, NZC, FACES), F32),
            pltpu.VMEM((NY, 2, NZC, FACES), F32),
            pltpu.VMEM((NY, 2, NZC, FACES), F32),
            pltpu.VMEM((NY, 2, NZC, FACES), F32),
            pltpu.VMEM((NZC, 2, NY, FACES), F32),
            pltpu.VMEM((NZC, 2, NY, FACES), F32),
            pltpu.VMEM((256, 128), F32),
            pltpu.VMEM((256, FACES), F32),
            pltpu.VMEM((PARTNERS, 256, 256), BF16),
            pltpu.VMEM((PARTNERS, 256, 256), BF16),
            pltpu.VMEM((PARTNERS, 256, FACES), F32),
            pltpu.VMEM((CH, PARTNERS, 256, FACES), F32),
            pltpu.VMEM((256, PARTNERS * FACES), BF16),
            pltpu.VMEM((128, PARTNERS * FACES), BF16),
            pltpu.VMEM((PARTNERS, 256, FACES), BF16),
            pltpu.VMEM((PARTNERS, 128, FACES), BF16),
            pltpu.VMEM((3, NZC, NY, CH, FACES), F32),
            pltpu.VMEM((3, NZC, NY, CH, FACES), F32),
            pltpu.VMEM((3, NY, NZC, CH, FACES), F32),
            pltpu.VMEM((3, NY, NZC, CH, FACES), F32),
            pltpu.VMEM((3, NY, NZC, CH, FACES), F32),
            pltpu.VMEM((3, NZC, NY, CH, FACES), F32),
            pltpu.VMEM((ROWS, FACES), F32),
            pltpu.VMEM((REPS, ROWS, FACES), F32),
            pltpu.SemaphoreType.DMA((3, 6)),
            pltpu.SemaphoreType.DMA((3, 6)),
            pltpu.SemaphoreType.DMA((3,)),
            pltpu.SemaphoreType.DMA((16,)),
            pltpu.SemaphoreType.DMA((16,)),
            pltpu.SemaphoreType.DMA((16,)),
        ],
        compiler_params=pltpu.CompilerParams(
            collective_id=0, has_side_effects=True, vmem_limit_bytes=60 * 1024 * 1024
        ),
        name="contact",
    )(
        surface_state.reshape(ROWS, FACES),
        direction.reshape(ROWS, FACES),
        stiffness,
        partners,
        contact_owner.reshape(1, BLOCKS),
        projection,
        mortar,
    )
    return result.reshape(BLOCKS, CH, FACES)


def solution(mesh):
    placed = (
        P("vol", "rep", None),
        P("vol", "rep", None),
        P("vol", None),
        P("vol", None),
        P("vol"),
        P(),
        P(),
    )
    return jax.shard_map(
        local, mesh=mesh, in_specs=placed, out_specs=P("vol", "rep", None), check_vma=False
    )
```

```python
import jax
import jax.numpy as jnp
from jax import lax
from jax.experimental import pallas as pl
from jax.experimental.pallas import tpu as pltpu
from jax.sharding import PartitionSpec as P

SHARPNESS = 1.5
BLOCKS = 112
CH = 8
FACES = 128
REPS = 4
NY = 8
NZ = 8
PARTNERS = 4
ROWS = BLOCKS * CH
SLOTS = 128
F32 = jnp.float32
BF16 = jnp.bfloat16
MESH = pl.DeviceIdType.MESH


def split(x):
    high = x.astype(BF16)
    return high, (x - high.astype(F32)).astype(BF16)


def dot(a, b):
    return jnp.dot(a, b, preferred_element_type=F32)


def body(
    state,
    move,
    stiff_in,
    partners_in,
    owner_in,
    proj,
    mortar_in,
    out,
    gs,
    go,
    gd,
    gr,
    gm,
    raw,
    orow,
    lab_t,
    lab,
    sti,
    pick,
    pick_t,
    prj,
    prd,
    mp,
    mq,
    ms,
    labs,
    stis,
    g,
    gta,
    wfs,
    wts,
    uhl,
    tan,
    mm,
    ml,
    mth,
    mtl,
    p,
    q,
    o,
    x_send,
    x_recv,
    x_local,
    c_send,
    c_recv,
    c_local,
):
    vol = lax.axis_index("vol")
    rep = lax.axis_index("rep")
    y = vol // 16
    z = lax.rem(vol // 2, NZ)
    core = lax.rem(vol, 2)
    right = lax.rem(rep + 1, REPS)
    left = lax.rem(rep + 3, REPS)

    def along_z(peer, cross):
        return y * 16 + peer * 2 + (1 - core if cross else core)

    def along_y(peer):
        return peer * 16 + z * 2 + core

    local_s = pltpu.make_async_copy(state, gs.at[rep], x_local.at[0])
    local_s.start()
    local_d = pltpu.make_async_copy(move, raw.at[pl.ds(0, ROWS)], x_local.at[1])
    local_d.start()
    barrier = pltpu.get_barrier_semaphore()
    for side in (right, left):
        pl.semaphore_signal(barrier, inc=1, device_id=(vol, side), device_id_type=MESH)

    def greet(o, carry):
        for peer in (
            along_z(lax.rem(z + o, NZ), False),
            along_z(lax.rem(z + o, NZ), True),
            along_y(lax.rem(y + o, NY)),
        ):
            pl.semaphore_signal(barrier, inc=1, device_id=(peer, rep), device_id_type=MESH)
        return carry

    pl.semaphore_signal(barrier, inc=1, device_id=(along_z(z, True), rep), device_id_type=MESH)
    lax.fori_loop(1, 8, greet, 0)

    lane = lax.broadcasted_iota(jnp.int32, (128, 128), 1)
    row = lax.broadcasted_iota(jnp.int32, (128, 128), 0)
    orow[...] = jnp.full((8, 128), -1.0, F32)
    orow[0:1, 0:BLOCKS] = owner_in[...].astype(F32)
    across = jnp.broadcast_to(orow[0:1, :], (128, 128))
    down = across.T
    rank = jnp.sum(jnp.where((across == down) & (row < lane), 1.0, 0.0), axis=0, keepdims=True)
    major = lax.rem(row // 8, 8)
    minor = lax.rem(row, 8)
    dest = jnp.where(
        row < 64, minor * 16 + major * 2 + core, major * 16 + minor * 2 + (1 - core)
    ).astype(F32)
    for h in range(2):
        chosen = jnp.where((across == dest) & (rank == float(h)), 1.0, 0.0)
        pick[h * 128 : (h + 1) * 128, 0:128] = chosen.astype(BF16)
        pick[h * 128 : (h + 1) * 128, 128:256] = chosen.astype(BF16)
        pick_t[:, h * 128 : (h + 1) * 128] = chosen.T.astype(BF16)

    def x_copy(src, dst, n, index, side):
        copy = pltpu.make_async_remote_copy(
            src_ref=src,
            dst_ref=dst,
            send_sem=x_send.at[n, index],
            recv_sem=x_recv.at[n, index],
            device_id=(vol, side),
            device_id_type=MESH,
        )
        copy.start()
        return copy

    def x_start(own, view, n):
        return [
            x_copy(own(0), view(rep, 0), n, 0, right),
            x_copy(own(1), view(rep, 1), n, 1, left),
            x_copy(own(1), view(rep, 1), n, 2, right),
            x_copy(own(0), view(rep, 0), n, 3, left),
        ]

    def x_relay(view, n, copies):
        copies[0].wait_recv()
        copies.append(x_copy(view(left, 0), view(left, 0), n, 4, right))
        copies[1].wait_recv()
        copies.append(x_copy(view(right, 1), view(right, 1), n, 5, left))

    def x_finish(copies):
        for copy in copies[2:]:
            copy.wait_recv()

    def phase(dim, cross, src, dst, sem):
        mine = z if dim == "z" else y

        def one(i, carry):
            peer = lax.rem(mine + i, 8)
            device = along_z(peer, cross) if dim == "z" else along_y(peer)
            pltpu.make_async_remote_copy(
                src_ref=src(peer),
                dst_ref=dst(mine),
                send_sem=c_send.at[sem],
                recv_sem=c_recv.at[sem],
                device_id=(device, rep),
                device_id_type=MESH,
            ).start()
            return carry

        lax.fori_loop(0 if cross else 1, 8, one, 0)
        if cross:
            return None
        own = pltpu.make_async_copy(src(mine), dst(mine), c_local.at[sem])
        own.start()
        return own

    def drain(own, ref, sem):
        count = 8 if own is None else 7
        whole = pltpu.make_async_remote_copy(
            src_ref=ref.at[pl.ds(0, count)],
            dst_ref=ref.at[pl.ds(0, count)],
            send_sem=c_send.at[sem],
            recv_sem=c_recv.at[sem],
            device_id=(vol, right),
            device_id_type=MESH,
        )
        if own is not None:
            own.wait()
        whole.wait_recv()
        whole.wait_send()

    def there_one(n):
        a = phase("z", False, lambda i: p.at[n, 0, i], lambda i: q.at[n, 0, i], 4 * n)
        b = phase("y", False, lambda i: p.at[n, 1, i], lambda i: q.at[n, 1, i], 4 * n + 1)
        return a, b

    def there_two(n, run, land):
        drain(run[0], q.at[n, 0], 4 * n)
        a = phase("y", False, lambda i: q.at[n, 0, :, i], lambda i: land(0).at[i], 4 * n + 2)
        drain(run[1], q.at[n, 1], 4 * n + 1)
        b = phase("z", True, lambda i: q.at[n, 1, :, i], lambda i: land(1).at[i], 4 * n + 3)
        return a, b

    def there_end(n, run, land):
        drain(run[0], land(0), 4 * n + 2)
        drain(run[1], land(1), 4 * n + 3)

    def back_one(n):
        a = phase("y", False, lambda i: p.at[n, 0, i], lambda i: q.at[n, 0, i], 4 * n)
        b = phase("z", True, lambda i: p.at[n, 1, i], lambda i: q.at[n, 1, i], 4 * n + 1)
        return a, b

    def back_two(n, run):
        drain(run[0], q.at[n, 0], 4 * n)
        a = phase("z", False, lambda i: q.at[n, 0, :, i], lambda i: o.at[n, 0, i], 4 * n + 2)
        drain(run[1], q.at[n, 1], 4 * n + 1)
        b = phase("y", False, lambda i: q.at[n, 1, :, i], lambda i: o.at[n, 1, i], 4 * n + 3)
        return a, b

    def back_end(n, run):
        drain(run[0], o.at[n, 0], 4 * n + 2)
        drain(run[1], o.at[n, 1], 4 * n + 3)

    def put(n, i, rows):
        for part in range(2):
            dst = p.at[n, part].reshape(64 * CH, FACES)
            dst[pl.ds(i, 64, stride=CH), :] = rows[part * 64 : (part + 1) * 64]

    def chosen_rows(rows, x):
        high, low = split(x)
        return dot(rows, jnp.concatenate([high, low], axis=0))

    def gs_view(origin, part):
        return gs.at[origin, pl.ds(part * (ROWS // 2), ROWS // 2)]

    def go_view(origin, part):
        return go.at[origin, pl.ds(part * (ROWS // 2), ROWS // 2)]

    def gr_view(origin, part):
        return gr.at[origin, pl.ds(part * 64 * CH, 64 * CH)]

    def gm_view(origin, part):
        return gm.at[origin, part]

    def gd_view(h):
        return lambda origin, part: gd.at[h, part, origin]

    pl.semaphore_wait(barrier, 24)
    x_state = x_start(
        lambda part: state.at[pl.ds(part * (ROWS // 2), ROWS // 2)], gs_view, 0
    )

    lab_t[...] = jnp.zeros((128, 128), F32)
    lab_t[0:PARTNERS, 0:BLOCKS] = (partners_in[...] + 1).astype(F32)
    count = lax.broadcasted_iota(jnp.int32, (1, 128), 1)
    lab_t[PARTNERS : PARTNERS + 1, :] = jnp.where(
        count < BLOCKS, count + (vol * BLOCKS + 1), 0
    ).astype(F32)
    lab[...] = lab_t[...].T
    sti[...] = jnp.zeros((128, FACES), F32)
    sti[0:BLOCKS, :] = stiff_in[...]
    table = jnp.where(lax.rem(rep, 2) == 0, sti[...], lab[...])
    rows = chosen_rows(pick[pl.ds((rep // 2) * 128, 128), :], table)
    for part in range(2):
        for i in range(8):
            mp[part, i] = rows[part * 64 + i * 8 : part * 64 + (i + 1) * 8]
    meta = (
        phase("z", False, lambda i: mp.at[0, i], lambda i: mq.at[0, i], 24),
        phase("y", False, lambda i: mp.at[1, i], lambda i: mq.at[1, i], 25),
    )

    raw[ROWS:, :] = jnp.zeros((128 * CH - ROWS, FACES), F32)
    local_d.wait()
    runs = []
    for h in range(2):
        for i in range(CH):
            x = raw[pl.ds(i, 128, stride=CH), :]
            put(h, i, chosen_rows(pick[h * 128 : (h + 1) * 128, :], x))
        runs.append(there_one(h))

    drain(meta[0], mq.at[0], 24)
    drain(meta[1], mq.at[1], 25)
    for part in range(2):
        flat = mq.at[part].reshape(64, FACES)
        for i in range(8):
            ms[part, i] = flat[pl.ds(i, 8, stride=8), :]
    meta = (
        phase("y", False, lambda i: ms.at[0, i], lambda i: gm.at[rep, 0, i], 26),
        phase("z", True, lambda i: ms.at[1, i], lambda i: gm.at[rep, 1, i], 27),
    )
    x_relay(gs_view, 0, x_state)

    for k in range(PARTNERS):
        cols = slice(k * FACES, (k + 1) * FACES)
        high, low = split(mortar_in[k])
        mm[0:FACES, cols] = high
        mm[FACES : 2 * FACES, cols] = high
        ml[:, cols] = low
        high, low = split(mortar_in[k].T)
        mth[k, 0:FACES, :] = high
        mth[k, FACES : 2 * FACES, :] = high
        mtl[k] = low
    prj[...] = jnp.zeros((CH, 128, FACES), F32)

    def land_d(h):
        return lambda part: gd.at[h, part, rep]

    runs[0] = there_two(0, runs[0], land_d(0))
    drain(meta[0], gm.at[rep, 0], 26)
    drain(meta[1], gm.at[rep, 1], 27)
    x_meta = x_start(lambda part: gm.at[rep, part], gm_view, 1)
    runs[1] = there_two(1, runs[1], land_d(1))
    there_end(0, runs[0], land_d(0))
    x_d0 = x_start(lambda part: gd.at[0, part, rep], gd_view(0), 2)

    def project(load, count, transposed, base):
        total = [jnp.zeros((count, FACES), F32) for _ in range(4)]
        for j in range(REPS * CH):
            x = load(j)
            for i in range(4):
                if transposed:
                    factor = proj[j, rep * CH + base + i]
                else:
                    factor = proj[rep * CH + base + i, j]
                total[i] = total[i] + factor * x
        return total

    def rows_of(ref, start):
        return lambda j: ref[j // CH, pl.ds(start * CH + j % CH, 56, stride=CH), :]

    x_finish(x_state)
    local_s.wait()
    for start in (0, 56):
        for base in (0, 4):
            total = project(rows_of(gs, start), 56, False, base)
            for i in range(4):
                prj[base + i, start : start + 56, :] = total[i]
    for h in range(2):
        for i in range(CH):
            put(2 + h, i, chosen_rows(pick[h * 128 : (h + 1) * 128, :], prj[i]))
        runs.append(there_one(2 + h))

    x_relay(gm_view, 1, x_meta)
    x_finish(x_meta)
    for h in range(2):
        stis[h * 128 : (h + 1) * 128] = gm.at[2 * h].reshape(128, FACES)[...]
        labs[h * 128 : (h + 1) * 128] = gm.at[2 * h + 1].reshape(128, FACES)[...]
    labels = labs[...]
    turned = labels.T
    ones = jnp.ones((256, FACES), BF16)
    for k in range(PARTNERS):
        hit = labels[:, k : k + 1] == turned[PARTNERS : PARTNERS + 1, :]
        g[k] = jnp.where(hit, 1.0, 0.0).astype(BF16)
        hit = labels[:, PARTNERS : PARTNERS + 1] == turned[k : k + 1, :]
        gta[:, k * 256 : (k + 1) * 256] = jnp.where(hit, 1.0, 0.0).astype(BF16)
        wfs[k] = dot(g[k], ones) * stis[...] * SHARPNESS

    x_relay(gd_view(0), 2, x_d0)
    there_end(1, runs[1], land_d(1))
    x_d1 = x_start(lambda part: gd.at[1, part, rep], gd_view(1), 3)

    def land(n):
        return lambda part: o.at[n, part]

    runs[2] = there_two(2, runs[2], land(2))

    def project_slots(h):
        for part in range(2):

            def load(j):
                flat = gd.at[h, part, j // CH].reshape(64 * CH, FACES)
                return flat[pl.ds(j % CH, 64, stride=CH), :]

            for base in (0, 4):
                total = project(load, 64, False, base)
                start = h * 128 + part * 64
                for i in range(4):
                    prd[base + i, start : start + 64, :] = total[i]

    x_finish(x_d0)
    project_slots(0)
    runs[3] = there_two(3, runs[3], land(3))
    x_relay(gd_view(1), 3, x_d1)

    def mapped(x):
        high, low = split(x)
        total = dot(jnp.concatenate([high, low], axis=1), mm[...]) + dot(high, ml[...])
        result = []
        for k in range(PARTNERS):
            high, low = split(total[:, k * FACES : (k + 1) * FACES])
            both = dot(g[k], jnp.concatenate([high, low], axis=1))
            result.append(both[:, 0:FACES] + both[:, FACES:])
        return result

    def weigh(i, carry):
        x = jnp.concatenate(
            [
                o.at[2 + h, part].reshape(64 * CH, FACES)[pl.ds(i, 64, stride=CH), :]
                for h in range(2)
                for part in range(2)
            ],
            axis=0,
        )
        for k, partner in enumerate(mapped(x)):
            squashed = 1.0 / (1.0 + jnp.exp(-SHARPNESS * (x - partner)))
            wts[i, k] = wfs[k] * squashed * (1.0 - squashed)
        return carry

    there_end(2, runs[2], land(2))
    there_end(3, runs[3], land(3))
    lax.fori_loop(0, CH, weigh, 0)
    x_finish(x_d1)
    project_slots(1)

    def pull(i, carry):
        x = prd[i]
        total = jnp.zeros((256, FACES), F32)
        for k, partner in enumerate(mapped(x)):
            traction = wts[i, k] * (x - partner)
            total = total + traction
            high, low = split(traction)
            pulled = dot(jnp.concatenate([high, low], axis=1), mth[k]) + dot(high, mtl[k])
            high, low = split(pulled)
            uhl[i, k * 256 : (k + 1) * 256, :] = jnp.concatenate([high, low], axis=1)
        tan[i] = total
        return carry

    def summed(i, h):
        both = dot(gta[h * 128 : (h + 1) * 128, :], uhl[i])
        return tan[i, h * 128 : (h + 1) * 128, :] - both[:, 0:FACES] - both[:, FACES:]

    lax.fori_loop(0, CH, pull, 0)
    mine = gr.at[rep]
    for i in range(CH):
        mine[pl.ds(i, 128, stride=CH), :] = summed(i, 1)
    x_back = x_start(lambda part: gr_view(rep, part), gr_view, 4)
    for i in range(CH):
        put(4, i, summed(i, 0))
    run_first = back_one(4)
    x_relay(gr_view, 4, x_back)
    run_first = back_two(4, run_first)
    x_finish(x_back)
    for part in range(2):

        def load(j):
            return gr[j // CH, pl.ds(part * 64 * CH + j % CH, 64, stride=CH), :]

        dst = p.at[5, part].reshape(64 * CH, FACES)
        for base in (0, 4):
            total = project(load, 64, True, base)
            for i in range(4):
                dst[pl.ds(base + i, 64, stride=CH), :] = total[i]
    run_second = back_one(5)
    back_end(4, run_first)

    def home(n, i):
        x = jnp.concatenate(
            [
                o.at[n, part].reshape(64 * CH, FACES)[pl.ds(i, 64, stride=CH), :]
                for part in range(2)
            ],
            axis=0,
        )
        high, low = split(x)
        h = n - 4
        both = dot(pick_t[:, h * 128 : (h + 1) * 128], jnp.concatenate([high, low], axis=1))
        return (both[:, 0:FACES] + both[:, FACES:])[0:BLOCKS]

    mine = go.at[rep]
    for i in range(CH):
        mine[pl.ds(i, BLOCKS, stride=CH), :] = home(4, i)
    x_home = x_start(lambda part: go_view(rep, part), go_view, 5)
    run_second = back_two(5, run_second)
    x_relay(go_view, 5, x_home)
    back_end(5, run_second)
    for i in range(CH):
        prj[i, 0:BLOCKS, :] = home(5, i)
    x_finish(x_home)
    for start in (0, 56):
        for base in (0, 4):
            total = project(rows_of(go, start), 56, True, base)
            for i in range(4):
                out[pl.ds(start * CH + base + i, 56, stride=CH), :] = (
                    total[i] + prj[base + i, start : start + 56, :]
                )
    for copy in x_state + x_meta + x_d0 + x_d1 + x_back + x_home:
        copy.wait_send()


def local(surface_state, direction, stiffness, partners, contact_owner, projection, mortar):
    vmem = pl.BlockSpec(memory_space=pltpu.VMEM)
    anywhere = pl.BlockSpec(memory_space=pl.ANY)
    result = pl.pallas_call(
        body,
        out_shape=jax.ShapeDtypeStruct((ROWS, FACES), F32),
        in_specs=[
            anywhere,
            anywhere,
            vmem,
            vmem,
            vmem,
            pl.BlockSpec(memory_space=pltpu.SMEM),
            vmem,
        ],
        out_specs=vmem,
        scratch_shapes=[
            pltpu.VMEM((REPS, ROWS, FACES), F32),
            pltpu.VMEM((REPS, ROWS, FACES), F32),
            pltpu.VMEM((2, 2, REPS, 8, 8, CH, FACES), F32),
            pltpu.VMEM((REPS, SLOTS * CH, FACES), F32),
            pltpu.VMEM((REPS, 2, 8, 8, FACES), F32),
            pltpu.VMEM((128 * CH, FACES), F32),
            pltpu.VMEM((8, 128), F32),
            pltpu.VMEM((128, 128), F32),
            pltpu.VMEM((128, 128), F32),
            pltpu.VMEM((128, FACES), F32),
            pltpu.VMEM((256, 256), BF16),
            pltpu.VMEM((128, 256), BF16),
            pltpu.VMEM((CH, 128, FACES), F32),
            pltpu.VMEM((CH, 256, FACES), F32),
            pltpu.VMEM((2, 8, 8, FACES), F32),
            pltpu.VMEM((2, 8, 8, FACES), F32),
            pltpu.VMEM((2, 8, 8, FACES), F32),
            pltpu.VMEM((256, 128), F32),
            pltpu.VMEM((256, FACES), F32),
            pltpu.VMEM((PARTNERS, 256, 256), BF16),
            pltpu.VMEM((256, PARTNERS * 256), BF16),
            pltpu.VMEM((PARTNERS, 256, FACES), F32),
            pltpu.VMEM((CH, PARTNERS, 256, FACES), F32),
            pltpu.VMEM((CH, PARTNERS * 256, 256), BF16),
            pltpu.VMEM((CH, 256, FACES), F32),
            pltpu.VMEM((256, PARTNERS * FACES), BF16),
            pltpu.VMEM((128, PARTNERS * FACES), BF16),
            pltpu.VMEM((PARTNERS, 256, FACES), BF16),
            pltpu.VMEM((PARTNERS, 128, FACES), BF16),
            pltpu.VMEM((6, 2, 8, 8, CH, FACES), F32),
            pltpu.VMEM((6, 2, 8, 8, CH, FACES), F32),
            pltpu.VMEM((6, 2, 8, 8, CH, FACES), F32),
            pltpu.SemaphoreType.DMA((6, 6)),
            pltpu.SemaphoreType.DMA((6, 6)),
            pltpu.SemaphoreType.DMA((2,)),
            pltpu.SemaphoreType.DMA((28,)),
            pltpu.SemaphoreType.DMA((28,)),
            pltpu.SemaphoreType.DMA((28,)),
        ],
        compiler_params=pltpu.CompilerParams(
            collective_id=0, has_side_effects=True, vmem_limit_bytes=60 * 1024 * 1024
        ),
        name="contact",
    )(
        surface_state.reshape(ROWS, FACES),
        direction.reshape(ROWS, FACES),
        stiffness,
        partners.T,
        contact_owner.reshape(1, BLOCKS),
        projection,
        mortar,
    )
    return result.reshape(BLOCKS, CH, FACES)


def solution(mesh):
    placed = (
        P("vol", "rep", None),
        P("vol", "rep", None),
        P("vol", None),
        P("vol", None),
        P("vol"),
        P(),
        P(),
    )
    return jax.shard_map(
        local, mesh=mesh, in_specs=placed, out_specs=P("vol", "rep", None), check_vma=False
    )
```

```python
import jax
import jax.numpy as jnp
from jax import lax
from jax.experimental import pallas as pl
from jax.experimental.pallas import tpu as pltpu
from jax.sharding import PartitionSpec as P

SHARPNESS = 1.5
BLOCKS = 112
CH = 8
FACES = 128
REPS = 4
NY = 8
NZ = 8
PARTNERS = 4
ROWS = BLOCKS * CH
SLOTS = 128
F32 = jnp.float32
BF16 = jnp.bfloat16
MESH = pl.DeviceIdType.MESH


def split(x):
    high = x.astype(BF16)
    return high, (x - high.astype(F32)).astype(BF16)


def dot(a, b):
    return jnp.dot(a, b, preferred_element_type=F32)


def body(
    state,
    move,
    stiff_in,
    partners_in,
    owner_in,
    proj,
    mortar_in,
    out,
    tb,
    tc,
    sp,
    dp,
    bk,
    hm,
    gm,
    raw,
    orow,
    lab_t,
    lab,
    sti,
    pick,
    pick_t,
    mp,
    mq,
    ms,
    labs,
    stis,
    g,
    gta,
    wfs,
    chg,
    uhl,
    tan,
    mm,
    ml,
    mth,
    mtl,
    p,
    q,
    o,
    x_send,
    x_recv,
    x_local,
    d_local,
    c_send,
    c_recv,
    c_local,
):
    vol = lax.axis_index("vol")
    rep = lax.axis_index("rep")
    y = vol // 16
    z = lax.rem(vol // 2, NZ)
    core = lax.rem(vol, 2)
    right = lax.rem(rep + 1, REPS)

    def along_z(peer, cross):
        return y * 16 + peer * 2 + (1 - core if cross else core)

    def along_y(peer):
        return peer * 16 + z * 2 + core

    local_d = pltpu.make_async_copy(move, raw.at[pl.ds(0, ROWS)], d_local)
    local_d.start()
    barrier = pltpu.get_barrier_semaphore()
    for side in (1, 3, 2):
        peer = lax.rem(rep + side, REPS)
        pl.semaphore_signal(barrier, inc=1, device_id=(vol, peer), device_id_type=MESH)

    def greet(o, carry):
        for peer in (
            along_z(lax.rem(z + o, NZ), False),
            along_z(lax.rem(z + o, NZ), True),
            along_y(lax.rem(y + o, NY)),
        ):
            pl.semaphore_signal(barrier, inc=1, device_id=(peer, rep), device_id_type=MESH)
        return carry

    pl.semaphore_signal(barrier, inc=1, device_id=(along_z(z, True), rep), device_id_type=MESH)
    lax.fori_loop(1, 8, greet, 0)

    lane = lax.broadcasted_iota(jnp.int32, (128, 128), 1)
    row = lax.broadcasted_iota(jnp.int32, (128, 128), 0)
    orow[...] = jnp.full((8, 128), -1.0, F32)
    orow[0:1, 0:BLOCKS] = owner_in[...].astype(F32)
    across = jnp.broadcast_to(orow[0:1, :], (128, 128))
    down = across.T
    rank = jnp.sum(jnp.where((across == down) & (row < lane), 1.0, 0.0), axis=0, keepdims=True)
    major = lax.rem(row // 8, 8)
    minor = lax.rem(row, 8)
    dest = jnp.where(
        row < 64, minor * 16 + major * 2 + core, major * 16 + minor * 2 + (1 - core)
    ).astype(F32)
    for h in range(2):
        chosen = jnp.where((across == dest) & (rank == float(h)), 1.0, 0.0)
        pick[h * 128 : (h + 1) * 128, 0:128] = chosen.astype(BF16)
        pick[h * 128 : (h + 1) * 128, 128:256] = chosen.astype(BF16)
        pick_t[:, h * 128 : (h + 1) * 128] = chosen.T.astype(BF16)

    def x_send_all(src, dst, n, base):
        copies = []
        for side in (1, 3, 2):
            peer = lax.rem(rep + side, REPS)
            copy = pltpu.make_async_remote_copy(
                src_ref=src(peer),
                dst_ref=dst,
                send_sem=x_send.at[n, base + side - 1],
                recv_sem=x_recv.at[n, base + side - 1],
                device_id=(vol, peer),
                device_id_type=MESH,
            )
            copy.start()
            copies.append(copy)
        return copies

    def turn_start(n, own, count):
        rows = count * CH
        dst = tb.at[n, rep, pl.ds(0, rows)]

        def quarter(peer):
            return own.at[pl.ds(peer * rows, rows)]

        copies = x_send_all(quarter, dst, n, 0)
        copy = pltpu.make_async_copy(quarter(rep), dst, x_local.at[n, 0])
        copy.start()
        return copies, copy

    def turn_middle(n, run, land, count, transposed):
        rows = count * CH
        for copy in run[0]:
            copy.wait_recv()
        run[1].wait()

        def share(r, carry):
            total = [jnp.zeros((count, FACES), F32) for _ in range(CH)]
            for j in range(REPS * CH):
                x = tb[n, j // CH, pl.ds(j % CH, count, stride=CH), :]
                for i in range(CH):
                    factor = proj[j, r * CH + i] if transposed else proj[r * CH + i, j]
                    total[i] = total[i] + factor * x
            for i in range(CH):
                tc[n, r, pl.ds(i, count, stride=CH), :] = total[i]
            return carry

        lax.fori_loop(0, REPS, share, 0)
        dst = land.at[pl.ds(rep * rows, rows)]

        def back(peer):
            return tc.at[n, peer, pl.ds(0, rows)]

        copies = x_send_all(back, dst, n, 3)
        copy = pltpu.make_async_copy(back(rep), dst, x_local.at[n, 1])
        copy.start()
        sent.extend(run[0] + copies)
        return copies, copy

    def turn_end(run):
        for copy in run[0]:
            copy.wait_recv()
        run[1].wait()

    sent = []

    def phase(dim, cross, src, dst, sem):
        mine = z if dim == "z" else y

        def one(i, carry):
            peer = lax.rem(mine + i, 8)
            device = along_z(peer, cross) if dim == "z" else along_y(peer)
            pltpu.make_async_remote_copy(
                src_ref=src(peer),
                dst_ref=dst(mine),
                send_sem=c_send.at[sem],
                recv_sem=c_recv.at[sem],
                device_id=(device, rep),
                device_id_type=MESH,
            ).start()
            return carry

        lax.fori_loop(0 if cross else 1, 8, one, 0)
        if cross:
            return None
        own = pltpu.make_async_copy(src(mine), dst(mine), c_local.at[sem])
        own.start()
        return own

    def drain(own, ref, sem):
        count = 8 if own is None else 7
        whole = pltpu.make_async_remote_copy(
            src_ref=ref.at[pl.ds(0, count)],
            dst_ref=ref.at[pl.ds(0, count)],
            send_sem=c_send.at[sem],
            recv_sem=c_recv.at[sem],
            device_id=(vol, right),
            device_id_type=MESH,
        )
        if own is not None:
            own.wait()
        whole.wait_recv()
        whole.wait_send()

    def there_one(n):
        a = phase("z", False, lambda i: p.at[n, 0, i], lambda i: q.at[n, 0, i], 4 * n)
        b = phase("y", False, lambda i: p.at[n, 1, i], lambda i: q.at[n, 1, i], 4 * n + 1)
        return a, b

    def there_two(n, run, land):
        drain(run[0], q.at[n, 0], 4 * n)
        a = phase("y", False, lambda i: q.at[n, 0, :, i], lambda i: land(0).at[i], 4 * n + 2)
        drain(run[1], q.at[n, 1], 4 * n + 1)
        b = phase("z", True, lambda i: q.at[n, 1, :, i], lambda i: land(1).at[i], 4 * n + 3)
        return a, b

    def there_end(n, run, land):
        drain(run[0], land(0), 4 * n + 2)
        drain(run[1], land(1), 4 * n + 3)

    def back_one(n):
        a = phase("y", False, lambda i: p.at[n, 0, i], lambda i: q.at[n, 0, i], 4 * n)
        b = phase("z", True, lambda i: p.at[n, 1, i], lambda i: q.at[n, 1, i], 4 * n + 1)
        return a, b

    def back_one_from(n, source):
        first = source.reshape(2, 8, 8, CH, FACES)
        a = phase("y", False, lambda i: first.at[0, i], lambda i: q.at[n, 0, i], 4 * n)
        b = phase("z", True, lambda i: first.at[1, i], lambda i: q.at[n, 1, i], 4 * n + 1)
        return a, b

    def back_two(n, run):
        drain(run[0], q.at[n, 0], 4 * n)
        a = phase("z", False, lambda i: q.at[n, 0, :, i], lambda i: o.at[n, 0, i], 4 * n + 2)
        drain(run[1], q.at[n, 1], 4 * n + 1)
        b = phase("y", False, lambda i: q.at[n, 1, :, i], lambda i: o.at[n, 1, i], 4 * n + 3)
        return a, b

    def back_end(n, run):
        drain(run[0], o.at[n, 0], 4 * n + 2)
        drain(run[1], o.at[n, 1], 4 * n + 3)

    def put(n, i, rows):
        for part in range(2):
            dst = p.at[n, part].reshape(64 * CH, FACES)
            dst[pl.ds(i, 64, stride=CH), :] = rows[part * 64 : (part + 1) * 64]

    def chosen_rows(rows, x):
        high, low = split(x)
        return dot(rows, jnp.concatenate([high, low], axis=0))

    pl.semaphore_wait(barrier, 25)
    turn_s = turn_start(0, state, BLOCKS // REPS)

    lab_t[...] = jnp.zeros((128, 128), F32)
    lab_t[0:PARTNERS, 0:BLOCKS] = (partners_in[...] + 1).astype(F32)
    count = lax.broadcasted_iota(jnp.int32, (1, 128), 1)
    lab_t[PARTNERS : PARTNERS + 1, :] = jnp.where(
        count < BLOCKS, count + (vol * BLOCKS + 1), 0
    ).astype(F32)
    lab[...] = lab_t[...].T
    sti[...] = jnp.zeros((128, FACES), F32)
    sti[0:BLOCKS, :] = stiff_in[...]
    table = jnp.where(lax.rem(rep, 2) == 0, sti[...], lab[...])
    rows = chosen_rows(pick[pl.ds((rep // 2) * 128, 128), :], table)
    for part in range(2):
        for i in range(8):
            mp[part, i] = rows[part * 64 + i * 8 : part * 64 + (i + 1) * 8]
    meta = (
        phase("z", False, lambda i: mp.at[0, i], lambda i: mq.at[0, i], 24),
        phase("y", False, lambda i: mp.at[1, i], lambda i: mq.at[1, i], 25),
    )

    raw[ROWS:, :] = jnp.zeros((128 * CH - ROWS, FACES), F32)
    local_d.wait()
    runs = []
    for h in range(2):
        for i in range(CH):
            x = raw[pl.ds(i, 128, stride=CH), :]
            put(h, i, chosen_rows(pick[h * 128 : (h + 1) * 128, :], x))
        runs.append(there_one(h))

    drain(meta[0], mq.at[0], 24)
    drain(meta[1], mq.at[1], 25)
    for part in range(2):
        flat = mq.at[part].reshape(64, FACES)
        for i in range(8):
            ms[part, i] = flat[pl.ds(i, 8, stride=8), :]
    meta = (
        phase("y", False, lambda i: ms.at[0, i], lambda i: gm.at[rep, 0, i], 26),
        phase("z", True, lambda i: ms.at[1, i], lambda i: gm.at[rep, 1, i], 27),
    )
    sp[ROWS:, :] = jnp.zeros((128 * CH - ROWS, FACES), F32)
    turn_s = turn_middle(0, turn_s, sp, BLOCKS // REPS, False)

    for k in range(PARTNERS):
        cols = slice(k * FACES, (k + 1) * FACES)
        high, low = split(mortar_in[k])
        mm[0:FACES, cols] = high
        mm[FACES : 2 * FACES, cols] = high
        ml[:, cols] = low
        high, low = split(mortar_in[k].T)
        mth[k, 0:FACES, :] = high
        mth[k, FACES : 2 * FACES, :] = high
        mtl[k] = low

    def land(n):
        return lambda part: o.at[n, part]

    def slots(n):
        return o.at[n].reshape(SLOTS * CH, FACES)

    runs[0] = there_two(0, runs[0], land(0))
    drain(meta[0], gm.at[rep, 0], 26)
    drain(meta[1], gm.at[rep, 1], 27)
    x_meta = x_send_all(lambda peer: gm.at[rep], gm.at[rep], 1, 0)
    sent.extend(x_meta)
    runs[1] = there_two(1, runs[1], land(1))
    turn_end(turn_s)
    for h in range(2):
        for i in range(CH):
            x = sp[pl.ds(i, 128, stride=CH), :]
            put(2 + h, i, chosen_rows(pick[h * 128 : (h + 1) * 128, :], x))
        runs.append(there_one(2 + h))
    there_end(0, runs[0], land(0))
    turn_0 = turn_start(2, slots(0), SLOTS // REPS)
    there_end(1, runs[1], land(1))
    turn_1 = turn_start(3, slots(1), SLOTS // REPS)

    for copy in x_meta:
        copy.wait_recv()
    for h in range(2):
        stis[h * 128 : (h + 1) * 128] = gm.at[2 * h].reshape(128, FACES)[...]
        labs[h * 128 : (h + 1) * 128] = gm.at[2 * h + 1].reshape(128, FACES)[...]
    labels = labs[...]
    turned = labels.T
    ones = jnp.ones((256, FACES), BF16)
    for k in range(PARTNERS):
        hit = labels[:, k : k + 1] == turned[PARTNERS : PARTNERS + 1, :]
        g[k] = jnp.where(hit, 1.0, 0.0).astype(BF16)
        hit = labels[:, PARTNERS : PARTNERS + 1] == turned[k : k + 1, :]
        gta[:, k * 256 : (k + 1) * 256] = jnp.where(hit, 1.0, 0.0).astype(BF16)
        wfs[k] = dot(g[k], ones) * stis[...] * SHARPNESS

    def dp_half(h):
        return dp.at[pl.ds(h * SLOTS * CH, SLOTS * CH)]

    turn_0 = turn_middle(2, turn_0, dp_half(0), SLOTS // REPS, False)
    runs[2] = there_two(2, runs[2], land(2))
    turn_1 = turn_middle(3, turn_1, dp_half(1), SLOTS // REPS, False)
    runs[3] = there_two(3, runs[3], land(3))

    def mapped(x):
        high, low = split(x)
        total = dot(jnp.concatenate([high, low], axis=1), mm[...]) + dot(high, ml[...])
        result = []
        for k in range(PARTNERS):
            high, low = split(total[:, k * FACES : (k + 1) * FACES])
            both = dot(g[k], jnp.concatenate([high, low], axis=1))
            result.append(both[:, 0:FACES] + both[:, FACES:])
        return result

    def change(i, carry):
        x = dp[pl.ds(i, 256, stride=CH), :]
        for k, partner in enumerate(mapped(x)):
            chg[i, k] = x - partner
        return carry

    def pull(i, carry):
        x = jnp.concatenate(
            [
                o.at[2 + h, part].reshape(64 * CH, FACES)[pl.ds(i, 64, stride=CH), :]
                for h in range(2)
                for part in range(2)
            ],
            axis=0,
        )
        total = jnp.zeros((256, FACES), F32)
        for k, partner in enumerate(mapped(x)):
            squashed = 1.0 / (1.0 + jnp.exp(-SHARPNESS * (x - partner)))
            traction = wfs[k] * squashed * (1.0 - squashed) * chg[i, k]
            total = total + traction
            high, low = split(traction)
            pulled = dot(jnp.concatenate([high, low], axis=1), mth[k]) + dot(high, mtl[k])
            high, low = split(pulled)
            uhl[i, k * 256 : (k + 1) * 256, :] = jnp.concatenate([high, low], axis=1)
        tan[i] = total
        return carry

    def summed(i, h):
        both = dot(gta[h * 128 : (h + 1) * 128, :], uhl[i])
        return tan[i, h * 128 : (h + 1) * 128, :] - both[:, 0:FACES] - both[:, FACES:]

    turn_end(turn_0)
    turn_end(turn_1)
    lax.fori_loop(0, CH, change, 0)
    there_end(2, runs[2], land(2))
    there_end(3, runs[3], land(3))
    lax.fori_loop(0, CH, pull, 0)
    for i in range(CH):
        bk[0, pl.ds(i, 128, stride=CH), :] = summed(i, 1)
    turn_b = turn_start(4, bk.at[0], SLOTS // REPS)
    for i in range(CH):
        put(4, i, summed(i, 0))
    run_first = back_one(4)
    run_second = turn_middle(4, turn_b, bk.at[1], SLOTS // REPS, True)
    run_first = back_two(4, run_first)
    turn_end(run_second)
    run_second = back_one_from(5, bk.at[1])
    back_end(4, run_first)

    def home(n, i):
        x = jnp.concatenate(
            [
                o.at[n, part].reshape(64 * CH, FACES)[pl.ds(i, 64, stride=CH), :]
                for part in range(2)
            ],
            axis=0,
        )
        high, low = split(x)
        h = n - 4
        both = dot(pick_t[:, h * 128 : (h + 1) * 128], jnp.concatenate([high, low], axis=1))
        return (both[:, 0:FACES] + both[:, FACES:])[0:BLOCKS]

    for i in range(CH):
        hm[0, pl.ds(i, BLOCKS, stride=CH), :] = home(4, i)
    turn_h = turn_start(5, hm.at[0], BLOCKS // REPS)
    run_second = back_two(5, run_second)
    turn_h = turn_middle(5, turn_h, hm.at[1], BLOCKS // REPS, True)
    back_end(5, run_second)
    late = [home(5, i) for i in range(CH)]
    turn_end(turn_h)
    for i in range(CH):
        out[pl.ds(i, BLOCKS, stride=CH), :] = hm[1, pl.ds(i, BLOCKS, stride=CH), :] + late[i]
    for copy in sent:
        copy.wait_send()


def local(surface_state, direction, stiffness, partners, contact_owner, projection, mortar):
    vmem = pl.BlockSpec(memory_space=pltpu.VMEM)
    anywhere = pl.BlockSpec(memory_space=pl.ANY)
    result = pl.pallas_call(
        body,
        out_shape=jax.ShapeDtypeStruct((ROWS, FACES), F32),
        in_specs=[
            anywhere,
            anywhere,
            vmem,
            vmem,
            vmem,
            pl.BlockSpec(memory_space=pltpu.SMEM),
            vmem,
        ],
        out_specs=vmem,
        scratch_shapes=[
            pltpu.VMEM((6, REPS, 32 * CH, FACES), F32),
            pltpu.VMEM((6, REPS, 32 * CH, FACES), F32),
            pltpu.VMEM((128 * CH, FACES), F32),
            pltpu.VMEM((2 * SLOTS * CH, FACES), F32),
            pltpu.VMEM((2, SLOTS * CH, FACES), F32),
            pltpu.VMEM((2, ROWS, FACES), F32),
            pltpu.VMEM((REPS, 2, 8, 8, FACES), F32),
            pltpu.VMEM((128 * CH, FACES), F32),
            pltpu.VMEM((8, 128), F32),
            pltpu.VMEM((128, 128), F32),
            pltpu.VMEM((128, 128), F32),
            pltpu.VMEM((128, FACES), F32),
            pltpu.VMEM((256, 256), BF16),
            pltpu.VMEM((128, 256), BF16),
            pltpu.VMEM((2, 8, 8, FACES), F32),
            pltpu.VMEM((2, 8, 8, FACES), F32),
            pltpu.VMEM((2, 8, 8, FACES), F32),
            pltpu.VMEM((256, 128), F32),
            pltpu.VMEM((256, FACES), F32),
            pltpu.VMEM((PARTNERS, 256, 256), BF16),
            pltpu.VMEM((256, PARTNERS * 256), BF16),
            pltpu.VMEM((PARTNERS, 256, FACES), F32),
            pltpu.VMEM((CH, PARTNERS, 256, FACES), F32),
            pltpu.VMEM((CH, PARTNERS * 256, 256), BF16),
            pltpu.VMEM((CH, 256, FACES), F32),
            pltpu.VMEM((256, PARTNERS * FACES), BF16),
            pltpu.VMEM((128, PARTNERS * FACES), BF16),
            pltpu.VMEM((PARTNERS, 256, FACES), BF16),
            pltpu.VMEM((PARTNERS, 128, FACES), BF16),
            pltpu.VMEM((6, 2, 8, 8, CH, FACES), F32),
            pltpu.VMEM((6, 2, 8, 8, CH, FACES), F32),
            pltpu.VMEM((6, 2, 8, 8, CH, FACES), F32),
            pltpu.SemaphoreType.DMA((6, 6)),
            pltpu.SemaphoreType.DMA((6, 6)),
            pltpu.SemaphoreType.DMA((6, 2)),
            pltpu.SemaphoreType.DMA,
            pltpu.SemaphoreType.DMA((28,)),
            pltpu.SemaphoreType.DMA((28,)),
            pltpu.SemaphoreType.DMA((28,)),
        ],
        compiler_params=pltpu.CompilerParams(
            collective_id=0, has_side_effects=True, vmem_limit_bytes=60 * 1024 * 1024
        ),
        name="contact",
    )(
        surface_state.reshape(ROWS, FACES),
        direction.reshape(ROWS, FACES),
        stiffness,
        partners.T,
        contact_owner.reshape(1, BLOCKS),
        projection,
        mortar,
    )
    return result.reshape(BLOCKS, CH, FACES)


def solution(mesh):
    placed = (
        P("vol", "rep", None),
        P("vol", "rep", None),
        P("vol", None),
        P("vol", None),
        P("vol"),
        P(),
        P(),
    )
    return jax.shard_map(
        local, mesh=mesh, in_specs=placed, out_specs=P("vol", "rep", None), check_vma=False
    )
```

```python
import jax
import jax.numpy as jnp
from jax import lax
from jax.experimental import pallas as pl
from jax.experimental.pallas import tpu as pltpu
from jax.sharding import PartitionSpec as P

SHARPNESS = 1.5
BLOCKS = 112
CH = 8
FACES = 128
REPS = 4
NY = 8
NZ = 8
PARTNERS = 4
ROWS = BLOCKS * CH
SLOTS = 128
F32 = jnp.float32
BF16 = jnp.bfloat16
MESH = pl.DeviceIdType.MESH


def split(x):
    high = x.astype(BF16)
    return high, (x - high.astype(F32)).astype(BF16)


def dot(a, b):
    return jnp.dot(a, b, preferred_element_type=F32)


def body(
    state,
    move,
    stiff_in,
    partners_in,
    owner_in,
    proj,
    mortar_in,
    out,
    tb,
    tc,
    sp,
    dp,
    bk,
    hm,
    gm,
    raw,
    orow,
    lab_t,
    lab,
    sti,
    pick,
    pick_t,
    mp,
    mq,
    ms,
    labs,
    stis,
    g,
    gta,
    wfs,
    chg,
    uhl,
    tan,
    mm,
    ml,
    mth,
    mtl,
    p,
    q,
    o,
    x_send,
    x_recv,
    x_local,
    d_local,
    c_send,
    c_recv,
    c_local,
):
    vol = lax.axis_index("vol")
    rep = lax.axis_index("rep")
    y = vol // 16
    z = lax.rem(vol // 2, NZ)
    core = lax.rem(vol, 2)
    right = lax.rem(rep + 1, REPS)

    def along_z(peer, cross):
        return y * 16 + peer * 2 + (1 - core if cross else core)

    def along_y(peer):
        return peer * 16 + z * 2 + core

    local_d = pltpu.make_async_copy(move, raw.at[pl.ds(0, ROWS)], d_local)
    local_d.start()
    barrier = pltpu.get_barrier_semaphore()
    for side in (1, 3, 2):
        peer = lax.rem(rep + side, REPS)
        pl.semaphore_signal(barrier, inc=1, device_id=(vol, peer), device_id_type=MESH)

    def greet(o, carry):
        for peer in (
            along_z(lax.rem(z + o, NZ), False),
            along_z(lax.rem(z + o, NZ), True),
            along_y(lax.rem(y + o, NY)),
        ):
            pl.semaphore_signal(barrier, inc=1, device_id=(peer, rep), device_id_type=MESH)
        return carry

    pl.semaphore_signal(barrier, inc=1, device_id=(along_z(z, True), rep), device_id_type=MESH)
    lax.fori_loop(1, 8, greet, 0)

    lane = lax.broadcasted_iota(jnp.int32, (128, 128), 1)
    row = lax.broadcasted_iota(jnp.int32, (128, 128), 0)
    orow[...] = jnp.full((8, 128), -1.0, F32)
    orow[0:1, 0:BLOCKS] = owner_in[...].astype(F32)
    across = jnp.broadcast_to(orow[0:1, :], (128, 128))
    down = across.T
    rank = jnp.sum(jnp.where((across == down) & (row < lane), 1.0, 0.0), axis=0, keepdims=True)
    parity = row // 64
    part_b = lax.rem(row // 32, 2)
    major = lax.rem(row // 4, 8)
    minor = 2 * lax.rem(row, 4) + lax.rem(y + z + major + parity, 2)
    dest = jnp.where(
        part_b == 0, minor * 16 + major * 2 + core, major * 16 + minor * 2 + (1 - core)
    ).astype(F32)
    plain_major = lax.rem(row // 8, 8)
    plain_minor = lax.rem(row, 8)
    plain = jnp.where(
        row < 64,
        plain_minor * 16 + plain_major * 2 + core,
        plain_major * 16 + plain_minor * 2 + (1 - core),
    ).astype(F32)
    for h in range(2):
        chosen = jnp.where((across == dest) & (rank == float(h)), 1.0, 0.0)
        pick[h * 128 : (h + 1) * 128, 0:128] = chosen.astype(BF16)
        pick[h * 128 : (h + 1) * 128, 128:256] = chosen.astype(BF16)
        pick_t[:, h * 128 : (h + 1) * 128] = chosen.T.astype(BF16)

    def x_send_all(src, dst, n, base):
        copies = []
        for side in (1, 3, 2):
            peer = lax.rem(rep + side, REPS)
            copy = pltpu.make_async_remote_copy(
                src_ref=src(peer),
                dst_ref=dst,
                send_sem=x_send.at[n, base + side - 1],
                recv_sem=x_recv.at[n, base + side - 1],
                device_id=(vol, peer),
                device_id_type=MESH,
            )
            copy.start()
            copies.append(copy)
        return copies

    def turn_start(n, own, count):
        rows = count * CH
        dst = tb.at[n, rep, pl.ds(0, rows)]

        def quarter(peer):
            return own.at[pl.ds(peer * rows, rows)]

        copies = x_send_all(quarter, dst, n, 0)
        copy = pltpu.make_async_copy(quarter(rep), dst, x_local.at[n, 0])
        copy.start()
        return copies, copy

    def turn_middle(n, run, land, count, transposed):
        rows = count * CH
        for copy in run[0]:
            copy.wait_recv()
        run[1].wait()

        def share(r, carry):
            total = [jnp.zeros((count, FACES), F32) for _ in range(CH)]
            for j in range(REPS * CH):
                x = tb[n, j // CH, pl.ds(j % CH, count, stride=CH), :]
                for i in range(CH):
                    factor = proj[j, r * CH + i] if transposed else proj[r * CH + i, j]
                    total[i] = total[i] + factor * x
            for i in range(CH):
                tc[n, r, pl.ds(i, count, stride=CH), :] = total[i]
            return carry

        lax.fori_loop(0, REPS, share, 0)
        dst = land.at[pl.ds(rep * rows, rows)]

        def back(peer):
            return tc.at[n, peer, pl.ds(0, rows)]

        copies = x_send_all(back, dst, n, 3)
        copy = pltpu.make_async_copy(back(rep), dst, x_local.at[n, 1])
        copy.start()
        sent.extend(run[0] + copies)
        return copies, copy

    def turn_end(run):
        for copy in run[0]:
            copy.wait_recv()
        run[1].wait()

    sent = []

    def phase(dim, cross, src, dst, sem):
        mine = z if dim == "z" else y

        def one(i, carry):
            peer = lax.rem(mine + i, 8)
            device = along_z(peer, cross) if dim == "z" else along_y(peer)
            pltpu.make_async_remote_copy(
                src_ref=src(peer),
                dst_ref=dst(mine),
                send_sem=c_send.at[sem],
                recv_sem=c_recv.at[sem],
                device_id=(device, rep),
                device_id_type=MESH,
            ).start()
            return carry

        lax.fori_loop(0 if cross else 1, 8, one, 0)
        if cross:
            return None
        own = pltpu.make_async_copy(src(mine), dst(mine), c_local.at[sem])
        own.start()
        return own

    def drain(own, ref, sem):
        count = 8 if own is None else 7
        whole = pltpu.make_async_remote_copy(
            src_ref=ref.at[pl.ds(0, count)],
            dst_ref=ref.at[pl.ds(0, count)],
            send_sem=c_send.at[sem],
            recv_sem=c_recv.at[sem],
            device_id=(vol, right),
            device_id_type=MESH,
        )
        if own is not None:
            own.wait()
        whole.wait_recv()
        whole.wait_send()

    def one(n, s, part, dim, cross, source):
        return phase(
            dim,
            cross,
            lambda i: source.at[s, part, i],
            lambda i: q.at[n, s, part, i // 2, lax.rem(i, 2)],
            8 * n + 4 * s + part,
        )

    def two(n, s, part, dim, cross):
        return phase(
            dim,
            cross,
            lambda i: q.at[n, s, part, :, lax.rem(i + y + z + s, 2), i // 2],
            lambda i: o.at[n, s, part, i],
            8 * n + 4 * s + 2 + part,
        )

    def there_one(n, s):
        source = p.at[n]
        return one(n, s, 0, "z", False, source), one(n, s, 1, "y", False, source)

    def there_two(n, s, run):
        drain(run[0], p.at[n, s, 0], 8 * n + 4 * s)
        a = two(n, s, 0, "y", False)
        drain(run[1], p.at[n, s, 1], 8 * n + 4 * s + 1)
        return a, two(n, s, 1, "z", True)

    def back_one(n, s, source):
        return one(n, s, 0, "y", False, source), one(n, s, 1, "z", True, source)

    def back_two(n, s, run):
        drain(run[0], p.at[n, s, 0], 8 * n + 4 * s)
        a = two(n, s, 0, "z", False)
        drain(run[1], p.at[n, s, 1], 8 * n + 4 * s + 1)
        return a, two(n, s, 1, "y", False)

    def end(n, s, run):
        for part in range(2):
            drain(run[part], o.at[n, s, part], 8 * n + 4 * s + 2 + part)

    def put(n, i, rows):
        p.at[n].reshape(SLOTS * CH, FACES)[pl.ds(i, SLOTS, stride=CH), :] = rows

    def chosen_rows(rows, x):
        high, low = split(x)
        return dot(rows, jnp.concatenate([high, low], axis=0))

    lab_t[...] = jnp.zeros((128, 128), F32)
    lab_t[0:PARTNERS, 0:BLOCKS] = (partners_in[...] + 1).astype(F32)
    count = lax.broadcasted_iota(jnp.int32, (1, 128), 1)
    lab_t[PARTNERS : PARTNERS + 1, :] = jnp.where(
        count < BLOCKS, count + (vol * BLOCKS + 1), 0
    ).astype(F32)
    lab[...] = lab_t[...].T
    sti[...] = jnp.zeros((128, FACES), F32)
    sti[0:BLOCKS, :] = stiff_in[...]
    table = jnp.where(lax.rem(rep, 2) == 0, sti[...], lab[...])
    plain_rank = (rep // 2).astype(F32)
    chosen = jnp.where((across == plain) & (rank == plain_rank), 1.0, 0.0).astype(BF16)
    rows = chosen_rows(jnp.concatenate([chosen, chosen], axis=1), table)
    for part in range(2):
        for i in range(8):
            mp[part, i] = rows[part * 64 + i * 8 : part * 64 + (i + 1) * 8]
    raw[ROWS:, :] = jnp.zeros((128 * CH - ROWS, FACES), F32)
    local_d.wait()
    for h in range(2):
        for i in range(CH):
            x = raw[pl.ds(i, 128, stride=CH), :]
            put(h, i, chosen_rows(pick[h * 128 : (h + 1) * 128, :], x))

    pl.semaphore_wait(barrier, 25)
    turn_s = turn_start(0, state, BLOCKS // REPS)

    meta = (
        phase("z", False, lambda i: mp.at[0, i], lambda i: mq.at[0, i], 48),
        phase("y", False, lambda i: mp.at[1, i], lambda i: mq.at[1, i], 49),
    )
    runs = [[there_one(n, s) for s in range(2)] for n in range(2)]

    drain(meta[0], mq.at[0], 48)
    drain(meta[1], mq.at[1], 49)
    for part in range(2):
        flat = mq.at[part].reshape(64, FACES)
        for i in range(8):
            ms[part, i] = flat[pl.ds(i, 8, stride=8), :]
    meta = (
        phase("y", False, lambda i: ms.at[0, i], lambda i: gm.at[rep, 0, i], 50),
        phase("z", True, lambda i: ms.at[1, i], lambda i: gm.at[rep, 1, i], 51),
    )
    sp[ROWS:, :] = jnp.zeros((128 * CH - ROWS, FACES), F32)
    turn_s = turn_middle(0, turn_s, sp, BLOCKS // REPS, False)

    for k in range(PARTNERS):
        cols = slice(k * FACES, (k + 1) * FACES)
        high, low = split(mortar_in[k])
        mm[0:FACES, cols] = high
        mm[FACES : 2 * FACES, cols] = high
        ml[:, cols] = low
        high, low = split(mortar_in[k].T)
        mth[k, 0:FACES, :] = high
        mth[k, FACES : 2 * FACES, :] = high
        mtl[k] = low

    def slots(n):
        return o.at[n].reshape(SLOTS * CH, FACES)

    runs[0] = [there_two(0, s, runs[0][s]) for s in range(2)]
    drain(meta[0], gm.at[rep, 0], 50)
    drain(meta[1], gm.at[rep, 1], 51)
    x_meta = x_send_all(lambda peer: gm.at[rep], gm.at[rep], 1, 0)
    sent.extend(x_meta)
    runs[1] = [there_two(1, s, runs[1][s]) for s in range(2)]
    turn_end(turn_s)
    for h in range(2):
        for i in range(CH):
            x = sp[pl.ds(i, 128, stride=CH), :]
            put(2 + h, i, chosen_rows(pick[h * 128 : (h + 1) * 128, :], x))
        runs.append([there_one(2 + h, s) for s in range(2)])
    for s in range(2):
        end(0, s, runs[0][s])
    turn_0 = turn_start(2, slots(0), SLOTS // REPS)
    for s in range(2):
        end(1, s, runs[1][s])
    turn_1 = turn_start(3, slots(1), SLOTS // REPS)

    for copy in x_meta:
        copy.wait_recv()
    turn_rows = jnp.where(lane == part_b * 64 + major * 8 + minor, 1.0, 0.0).astype(BF16)
    turn_rows = jnp.concatenate([turn_rows, turn_rows], axis=1)
    for h in range(2):
        stis[h * 128 : (h + 1) * 128] = chosen_rows(
            turn_rows, gm.at[2 * h].reshape(128, FACES)[...]
        )
        labs[h * 128 : (h + 1) * 128] = chosen_rows(
            turn_rows, gm.at[2 * h + 1].reshape(128, FACES)[...]
        )
    labels = labs[...]
    turned = labels.T
    ones = jnp.ones((256, FACES), BF16)
    for k in range(PARTNERS):
        hit = labels[:, k : k + 1] == turned[PARTNERS : PARTNERS + 1, :]
        g[k] = jnp.where(hit, 1.0, 0.0).astype(BF16)
        hit = labels[:, PARTNERS : PARTNERS + 1] == turned[k : k + 1, :]
        gta[:, k * 256 : (k + 1) * 256] = jnp.where(hit, 1.0, 0.0).astype(BF16)
        wfs[k] = dot(g[k], ones) * stis[...] * SHARPNESS

    def dp_half(h):
        return dp.at[pl.ds(h * SLOTS * CH, SLOTS * CH)]

    turn_0 = turn_middle(2, turn_0, dp_half(0), SLOTS // REPS, False)
    runs[2] = [there_two(2, s, runs[2][s]) for s in range(2)]
    turn_1 = turn_middle(3, turn_1, dp_half(1), SLOTS // REPS, False)
    runs[3] = [there_two(3, s, runs[3][s]) for s in range(2)]

    def mapped(x):
        high, low = split(x)
        total = dot(jnp.concatenate([high, low], axis=1), mm[...]) + dot(high, ml[...])
        result = []
        for k in range(PARTNERS):
            high, low = split(total[:, k * FACES : (k + 1) * FACES])
            both = dot(g[k], jnp.concatenate([high, low], axis=1))
            result.append(both[:, 0:FACES] + both[:, FACES:])
        return result

    def change(i, carry):
        x = dp[pl.ds(i, 256, stride=CH), :]
        for k, partner in enumerate(mapped(x)):
            chg[i, k] = x - partner
        return carry

    def pull(i, carry):
        x = jnp.concatenate(
            [slots(2 + h)[pl.ds(i, SLOTS, stride=CH), :] for h in range(2)],
            axis=0,
        )
        total = jnp.zeros((256, FACES), F32)
        for k, partner in enumerate(mapped(x)):
            squashed = 1.0 / (1.0 + jnp.exp(-SHARPNESS * (x - partner)))
            traction = wfs[k] * squashed * (1.0 - squashed) * chg[i, k]
            total = total + traction
            high, low = split(traction)
            pulled = dot(jnp.concatenate([high, low], axis=1), mth[k]) + dot(high, mtl[k])
            high, low = split(pulled)
            uhl[i, k * 256 : (k + 1) * 256, :] = jnp.concatenate([high, low], axis=1)
        tan[i] = total
        return carry

    def summed(i, h):
        both = dot(gta[h * 128 : (h + 1) * 128, :], uhl[i])
        return tan[i, h * 128 : (h + 1) * 128, :] - both[:, 0:FACES] - both[:, FACES:]

    turn_end(turn_0)
    turn_end(turn_1)
    lax.fori_loop(0, CH, change, 0)
    for h in range(2, 4):
        for s in range(2):
            end(h, s, runs[h][s])
    lax.fori_loop(0, CH, pull, 0)
    for i in range(CH):
        bk[0, pl.ds(i, 128, stride=CH), :] = summed(i, 1)
    part_rows = SLOTS * CH // 2

    def bk_half(k, s):
        return bk.at[k, pl.ds(s * part_rows, part_rows)]

    turn_b = [turn_start(4 + s, bk_half(0, s), SLOTS // REPS // 2) for s in range(2)]
    for i in range(CH):
        put(4, i, summed(i, 0))
    first = [back_one(4, s, p.at[4]) for s in range(2)]
    for s in range(2):
        turn_b[s] = turn_middle(4 + s, turn_b[s], bk_half(1, s), SLOTS // REPS // 2, True)
        first[s] = back_two(4, s, first[s])
    second = []
    for s in range(2):
        turn_end(turn_b[s])
        second.append(back_one(5, s, bk.at[1].reshape(2, 2, 8, 4, CH, FACES)))
    for s in range(2):
        end(4, s, first[s])

    def home(n, i):
        high, low = split(slots(n)[pl.ds(i, SLOTS, stride=CH), :])
        h = n - 4
        both = dot(pick_t[:, h * 128 : (h + 1) * 128], jnp.concatenate([high, low], axis=1))
        return (both[:, 0:FACES] + both[:, FACES:])[0:BLOCKS]

    def hm_half(k, s):
        return hm.at[k, pl.ds(s * (ROWS // 2), ROWS // 2)]

    for i in range(CH):
        hm[0, pl.ds(i, BLOCKS, stride=CH), :] = home(4, i)
    turn_h = [turn_start(6 + s, hm_half(0, s), BLOCKS // REPS // 2) for s in range(2)]
    for s in range(2):
        second[s] = back_two(5, s, second[s])
    for s in range(2):
        turn_h[s] = turn_middle(6 + s, turn_h[s], hm_half(1, s), BLOCKS // REPS // 2, True)
    for s in range(2):
        end(5, s, second[s])
    late = [home(5, i) for i in range(CH)]
    for s in range(2):
        turn_end(turn_h[s])
    for i in range(CH):
        out[pl.ds(i, BLOCKS, stride=CH), :] = hm[1, pl.ds(i, BLOCKS, stride=CH), :] + late[i]
    for copy in sent:
        copy.wait_send()


def local(surface_state, direction, stiffness, partners, contact_owner, projection, mortar):
    vmem = pl.BlockSpec(memory_space=pltpu.VMEM)
    anywhere = pl.BlockSpec(memory_space=pl.ANY)
    result = pl.pallas_call(
        body,
        out_shape=jax.ShapeDtypeStruct((ROWS, FACES), F32),
        in_specs=[
            anywhere,
            anywhere,
            vmem,
            vmem,
            vmem,
            pl.BlockSpec(memory_space=pltpu.SMEM),
            vmem,
        ],
        out_specs=vmem,
        scratch_shapes=[
            pltpu.VMEM((8, REPS, 32 * CH, FACES), F32),
            pltpu.VMEM((8, REPS, 32 * CH, FACES), F32),
            pltpu.VMEM((128 * CH, FACES), F32),
            pltpu.VMEM((2 * SLOTS * CH, FACES), F32),
            pltpu.VMEM((2, SLOTS * CH, FACES), F32),
            pltpu.VMEM((2, ROWS, FACES), F32),
            pltpu.VMEM((REPS, 2, 8, 8, FACES), F32),
            pltpu.VMEM((128 * CH, FACES), F32),
            pltpu.VMEM((8, 128), F32),
            pltpu.VMEM((128, 128), F32),
            pltpu.VMEM((128, 128), F32),
            pltpu.VMEM((128, FACES), F32),
            pltpu.VMEM((256, 256), BF16),
            pltpu.VMEM((128, 256), BF16),
            pltpu.VMEM((2, 8, 8, FACES), F32),
            pltpu.VMEM((2, 8, 8, FACES), F32),
            pltpu.VMEM((2, 8, 8, FACES), F32),
            pltpu.VMEM((256, 128), F32),
            pltpu.VMEM((256, FACES), F32),
            pltpu.VMEM((PARTNERS, 256, 256), BF16),
            pltpu.VMEM((256, PARTNERS * 256), BF16),
            pltpu.VMEM((PARTNERS, 256, FACES), F32),
            pltpu.VMEM((CH, PARTNERS, 256, FACES), F32),
            pltpu.VMEM((CH, PARTNERS * 256, 256), BF16),
            pltpu.VMEM((CH, 256, FACES), F32),
            pltpu.VMEM((256, PARTNERS * FACES), BF16),
            pltpu.VMEM((128, PARTNERS * FACES), BF16),
            pltpu.VMEM((PARTNERS, 256, FACES), BF16),
            pltpu.VMEM((PARTNERS, 128, FACES), BF16),
            pltpu.VMEM((6, 2, 2, 8, 4, CH, FACES), F32),
            pltpu.VMEM((6, 2, 2, 4, 2, 4, CH, FACES), F32),
            pltpu.VMEM((6, 2, 2, 8, 4, CH, FACES), F32),
            pltpu.SemaphoreType.DMA((8, 6)),
            pltpu.SemaphoreType.DMA((8, 6)),
            pltpu.SemaphoreType.DMA((8, 2)),
            pltpu.SemaphoreType.DMA,
            pltpu.SemaphoreType.DMA((52,)),
            pltpu.SemaphoreType.DMA((52,)),
            pltpu.SemaphoreType.DMA((52,)),
        ],
        compiler_params=pltpu.CompilerParams(
            collective_id=0, has_side_effects=True, vmem_limit_bytes=60 * 1024 * 1024
        ),
        name="contact",
    )(
        surface_state.reshape(ROWS, FACES),
        direction.reshape(ROWS, FACES),
        stiffness,
        partners.T,
        contact_owner.reshape(1, BLOCKS),
        projection,
        mortar,
    )
    return result.reshape(BLOCKS, CH, FACES)


def solution(mesh):
    placed = (
        P("vol", "rep", None),
        P("vol", "rep", None),
        P("vol", None),
        P("vol", None),
        P("vol"),
        P(),
        P(),
    )
    return jax.shard_map(
        local, mesh=mesh, in_specs=placed, out_specs=P("vol", "rep", None), check_vma=False
    )
```
